32 devices in a mesh: py: 4 (over z), px: 2 (over x), pz: 4 (over y, core).
Axes of the slice: x: 2, y: 2, z: 4, core: 2. Of those that a mesh axis runs over, the one named last changes fastest.
Arguments:
- density: float32 [32, 128, 128, 128], P('py', 'px', 'pz'), may hold values from 0.2 to 1.8
- crowding: float32 [32, 128, 128, 128], P('py', 'px', 'pz'), may hold values from 0.5 to 2
Outputs:
- column_sum: float32 [32, 128, 128, 128], P('py', 'px', 'pz')
- density_end: float32 [32, 128, 128, 128], P('py', 'px', 'pz')
The draws below stay inside these ranges and needn't reach their ends.
All inputs are finite; a program needn't handle non-finite values.
Results may differ from the reference program's by a relative error of at most 0.00002.
Values sent between devices are 32-bit elements; how exact they have to be, the bound alone decides.
A program may use at most 320 MiB of HBM per device.

```python
import jax
import jax.numpy as jnp
from jax import lax

GRID_Y = 32
GRID_X = 128
GRID_Z = 128
SPECIES = 128
STEPS = 6


def block_scale(stream_key, extent, cuts, low, largest):
    gain, own = 1.0, jax.random.fold_in(stream_key, 6)
    for position, parts in cuts:
        heights = jnp.exp(jax.random.uniform(jax.random.fold_in(own, position), (parts,), jnp.float32, low / len(cuts), largest / len(cuts)))
        gain = gain * jnp.repeat(heights, extent[position] // parts).reshape([-1 if axis == position else 1 for axis in range(len(extent))])
    return gain


def setup_inputs(seed: int = 0) -> dict:
    streams_of = jax.random.split(jax.random.key(seed), 3)
    return {
        "density": jnp.clip(0.2 + 1.5999999 * jax.random.uniform(streams_of[0], (GRID_Y, GRID_X, GRID_Z, SPECIES), jnp.float32) ** block_scale(streams_of[0], (GRID_Y, GRID_X, GRID_Z, SPECIES), ((0, 4), (1, 2), (2, 4)), -0.2, 0.2), 0.2, 1.8),
        "crowding": jnp.clip(0.5 + 1.5 * jax.random.uniform(streams_of[1], (GRID_Y, GRID_X, GRID_Z, SPECIES), jnp.float32) ** block_scale(streams_of[1], (GRID_Y, GRID_X, GRID_Z, SPECIES), ((0, 4), (1, 2), (2, 4)), -0.2, 0.2), 0.5, 2.0),
    }


def without_rim(values, dims):
    for dim in dims:
        values = lax.slice_in_dim(values, 1, values.shape[dim] - 1, axis=dim)
    return values


def shifted_cells(values, dim, start, dims):
    others = [other for other in dims if other != dim]
    values = without_rim(values, others)
    return lax.slice_in_dim(values, start, start + values.shape[dim] - 2, axis=dim)


def march_step(padded, crowding):
    middle = without_rim(padded, (0, 1, 2))
    lower = [shifted_cells(padded, dim, 0, (0, 1, 2)) for dim in (0, 1, 2)]
    upper = [shifted_cells(padded, dim, 2, (0, 1, 2)) for dim in (0, 1, 2)]
    spread = lower[0] + upper[0] + lower[1] + upper[1] + lower[2] + upper[2] - 6.0 * middle
    return middle + 0.1 * spread + 0.2 * middle * (1.0 - middle * crowding)


def reference(density, crowding):
    for step in range(STEPS):
        density = march_step(jnp.pad(density, ((1, 1), (1, 1), (1, 1), (0, 0)), mode="constant"), crowding)
    column_sum = jnp.cumsum(density, axis=0) / GRID_Y
    return column_sum, density
```

```python
import functools

import jax
import jax.numpy as jnp
from jax import lax
from jax.experimental import pallas as pl
from jax.experimental.pallas import tpu as pltpu
from jax.sharding import PartitionSpec as P

STEPS = 6
CHUNKS = 8
AXES = ("py", "px", "pz")
MESH = pl.DeviceIdType.MESH


def kernel(
    counts, chunks, density, crowding, odd, even,
    crowd, y_in, x_in, z_in, z_out, total_in, total_out,
    load_sem, y_send, y_recv, face_send, face_recv, total_send, total_recv,
):
    planes, rows, depth, lanes = density.shape
    part = rows // chunks
    last = planes - 1
    place = [lax.axis_index(axis) for axis in AXES]
    near = []
    for axis, at, count in zip(AXES, place, counts):
        near.append(((at > 0, {axis: at - 1}), (at < count - 1, {axis: at + 1})))
    groups = (pl.ds(0, 1), pl.ds(1, planes - 2), pl.ds(last, 1))

    barrier = pltpu.get_barrier_semaphore()
    awaited = jnp.int32(0)
    for sides in near:
        for there, device in sides:
            awaited = awaited + there.astype(jnp.int32)

            @pl.when(there)
            def _(device=device):
                pl.semaphore_signal(barrier, inc=1, device_id=device, device_id_type=MESH)

    load_field = pltpu.make_async_copy(density, even, load_sem.at[0])
    load_crowd = pltpu.make_async_copy(crowding, crowd, load_sem.at[1])
    load_field.start()
    load_crowd.start()
    pl.semaphore_wait(barrier, awaited)

    def field(level):
        return even if level % 2 == 0 else odd

    def y_copy(level, side, chunk):
        source = density if level == 0 else field(level)
        own = pl.ds(chunk * part, part)
        return pltpu.make_async_remote_copy(
            src_ref=source.at[last if side == 0 else 0, own],
            dst_ref=y_in.at[level, side, own],
            send_sem=y_send.at[level, side, chunk],
            recv_sem=y_recv.at[level, side, chunk],
            device_id=near[0][1 - side][1],
            device_id_type=MESH,
        )

    def face_copy(level, dim, side, group):
        own = groups[group]
        if dim == 1:
            source = density if level == 0 else field(level)
            source, landing = source.at[own, rows - 1 if side == 0 else 0], x_in
        else:
            source, landing = z_out.at[level, side, own], z_in
        slot = (level, (dim - 1) * 2 + side, group)
        return pltpu.make_async_remote_copy(
            src_ref=source,
            dst_ref=landing.at[level, side, own],
            send_sem=face_send.at[slot],
            recv_sem=face_recv.at[slot],
            device_id=near[dim][1 - side][1],
            device_id_type=MESH,
        )

    def total_copy(chunk):
        own = pl.ds(chunk * part, part)
        return pltpu.make_async_remote_copy(
            src_ref=total_out.at[own],
            dst_ref=total_in.at[own],
            send_sem=total_send.at[chunk],
            recv_sem=total_recv.at[chunk],
            device_id=near[0][1][1],
            device_id_type=MESH,
        )

    def sent_to(dim, side):
        return near[dim][1 - side][0]

    def comes_from(dim, side):
        return near[dim][side][0]

    def when(condition, action):
        pl.when(condition)(action)

    def y_start(level, chunk):
        for side in (0, 1):
            when(sent_to(0, side), lambda side=side: y_copy(level, side, chunk).start())

    def y_wait_send(level, chunk):
        for side in (0, 1):
            when(sent_to(0, side), lambda side=side: y_copy(level, side, chunk).wait_send())

    def y_wait_recv(level, chunk):
        for side in (0, 1):
            when(comes_from(0, side), lambda side=side: y_copy(level, side, chunk).wait_recv())

    def faces(level, some, dims, which, act):
        for dim in dims:
            for side in (0, 1):
                def action(dim=dim, side=side):
                    for group in some:
                        getattr(face_copy(level, dim, side, group), act)()

                when(which(dim, side), action)

    OUTER, INNER, ALL = (0, 2), (1,), (0, 2, 1)

    def over(low, high, body):
        lax.fori_loop(low, high, lambda i, carry: (body(i), carry)[1], 0)

    over(0, chunks, lambda chunk: y_start(0, chunk))
    faces(0, ALL, (1,), sent_to, "start")

    for side in (0, 1):
        @pl.when(jnp.logical_not(comes_from(0, side)))
        def _(side=side):
            def clear(row):
                for level in range(STEPS):
                    y_in[level, side, row] = jnp.zeros((depth, lanes), jnp.float32)
            over(0, rows, clear)

        @pl.when(jnp.logical_not(comes_from(1, side)))
        def _(side=side):
            def clear(plane):
                for level in range(STEPS):
                    x_in[level, side, plane] = jnp.zeros((depth, lanes), jnp.float32)
            over(0, planes, clear)

        @pl.when(jnp.logical_not(comes_from(2, side)))
        def _(side=side):
            def clear(plane):
                for level in range(STEPS):
                    z_in[level, side, plane] = jnp.zeros((rows, lanes), jnp.float32)
            over(0, planes, clear)

    load_field.wait()

    def pack(row):
        for plane in range(planes):
            z_out[0, 1, plane, pl.ds(row, 1)] = even[plane, row, 0:1]
            z_out[0, 0, plane, pl.ds(row, 1)] = even[plane, row, depth - 1:depth]

    over(0, rows, pack)
    faces(0, ALL, (2,), sent_to, "start")
    load_crowd.wait()

    index = lax.broadcasted_iota(jnp.int32, (depth, lanes), 0)
    at_low, at_high = index == 0, index == depth - 1

    def advance(level, plane, row, x_edge):
        now = field(level)
        middle = now[plane, row]
        below = y_in[level, 0, row] if plane == 0 else now[plane - 1, row]
        above = y_in[level, 1, row] if plane == last else now[plane + 1, row]
        before = x_in[level, 0, plane] if x_edge < 0 else now[plane, row - 1]
        after = x_in[level, 1, plane] if x_edge > 0 else now[plane, row + 1]
        down = jnp.where(at_low, z_in[level, 0, plane, pl.ds(row, 1)], pltpu.roll(middle, 1, 0))
        up = jnp.where(at_high, z_in[level, 1, plane, pl.ds(row, 1)], pltpu.roll(middle, depth - 1, 0))
        around = ((below + above) + (before + after)) + (down + up)
        rate = 6.0 - 2.0 * (middle * crowd[plane, row])
        value = 0.1 * (around + middle * rate)
        field(level + 1)[plane, row] = value
        if level + 1 < STEPS:
            z_out[level + 1, 1, plane, pl.ds(row, 1)] = value[0:1]
            z_out[level + 1, 0, plane, pl.ds(row, 1)] = value[depth - 1:depth]
        return value

    def sweep(low, high, body):
        when(low == 0, lambda: body(0, -1))
        over(jnp.maximum(low, 1), jnp.minimum(high, rows - 1), lambda row: body(row, 0))
        when(high == rows, lambda: body(rows - 1, 1))

    for level in range(STEPS - 1):
        faces(level, OUTER, (1, 2), comes_from, "wait_recv")
        if level:
            faces(level - 1, OUTER, (1, 2), sent_to, "wait_send")

        def outer(chunk, level=level):
            y_wait_recv(level, chunk)
            if level:
                y_wait_send(level - 1, chunk)

            def cells(row, x_edge):
                for plane in (0, last):
                    advance(level, plane, row, x_edge)

            sweep(chunk * part, (chunk + 1) * part, cells)
            y_start(level + 1, chunk)

        over(0, chunks, outer)
        faces(level + 1, OUTER, (1, 2), sent_to, "start")

        faces(level, INNER, (1, 2), comes_from, "wait_recv")
        if level:
            faces(level - 1, INNER, (1, 2), sent_to, "wait_send")

        def cells(row, x_edge, level=level):
            for plane in range(1, last):
                advance(level, plane, row, x_edge)

        sweep(jnp.int32(0), jnp.int32(rows), cells)
        faces(level + 1, INNER, (1, 2), sent_to, "start")

    final = STEPS - 1
    faces(final, ALL, (1, 2), comes_from, "wait_recv")
    faces(final - 1, ALL, (1, 2), sent_to, "wait_send")
    first, forwards = jnp.logical_not(near[0][0][0]), near[0][1][0]

    def ending(chunk):
        y_wait_recv(final, chunk)
        y_wait_send(final - 1, chunk)

        def cells(row, x_edge):
            total = advance(final, 0, row, x_edge)
            for plane in range(1, planes):
                total = total + advance(final, plane, row, x_edge)
            total_out[row] = total

        sweep(chunk * part, (chunk + 1) * part, cells)
        when(jnp.logical_and(first, forwards), lambda: total_copy(chunk).start())

    over(0, chunks, ending)
    faces(final, ALL, (1, 2), sent_to, "wait_send")
    over(0, chunks, lambda chunk: y_wait_send(final, chunk))

    @pl.when(first)
    def _():
        def clear(row):
            total_in[row] = jnp.zeros((depth, lanes), jnp.float32)
        over(0, rows, clear)

    result, scale = odd, 1.0 / (planes * counts[0])

    def summing(chunk):
        @pl.when(jnp.logical_not(first))
        def _():
            total_copy(chunk).wait_recv()

            @pl.when(forwards)
            def _():
                def add(row):
                    total_out[row] = total_out[row] + total_in[row]
                over(chunk * part, (chunk + 1) * part, add)
                total_copy(chunk).start()

        def cells(row):
            running = total_in[row]
            for plane in range(planes):
                running = running + even[plane, row]
                result[plane, row] = running * scale
        over(chunk * part, (chunk + 1) * part, cells)

    over(0, chunks, summing)
    when(forwards, lambda: over(0, chunks, lambda chunk: total_copy(chunk).wait_send()))


def local(mesh, density, crowding):
    planes, rows, depth, lanes = density.shape
    chunks = CHUNKS if rows % CHUNKS == 0 else 1
    counts = tuple(mesh.shape[axis] for axis in AXES)
    f32 = jnp.float32
    block = (planes, rows, depth, lanes)
    scratch = [
        (block), (STEPS, 2, rows, depth, lanes), (STEPS, 2, planes, depth, lanes),
        (STEPS, 2, planes, rows, lanes), (STEPS, 2, planes, rows, lanes),
        (rows, depth, lanes), (rows, depth, lanes),
    ]
    DMA = pltpu.SemaphoreType.DMA
    cells = planes * rows * depth * lanes
    return pl.pallas_call(
        functools.partial(kernel, counts, chunks),
        out_shape=(pltpu.VMEM(block, f32), pltpu.VMEM(block, f32)),
        in_specs=[pl.BlockSpec(memory_space=pltpu.HBM)] * 2,
        out_specs=(pl.BlockSpec(memory_space=pltpu.VMEM), pl.BlockSpec(memory_space=pltpu.VMEM)),
        scratch_shapes=[pltpu.VMEM(shape, f32) for shape in scratch] + [
            DMA((2,)),
            DMA((STEPS, 2, chunks)), DMA((STEPS, 2, chunks)),
            DMA((STEPS, 4, 3)), DMA((STEPS, 4, 3)),
            DMA((chunks,)), DMA((chunks,)),
        ],
        compiler_params=pltpu.CompilerParams(
            collective_id=0, has_side_effects=True, vmem_limit_bytes=40 * 2**20
        ),
        cost_estimate=pl.CostEstimate(flops=cells * 66, bytes_accessed=cells * 16, transcendentals=0),
        name="march",
    )(density, crowding)


def solution(mesh):
    spec = P(*AXES, None)
    return jax.shard_map(
        functools.partial(local, mesh), mesh=mesh, in_specs=(spec, spec), out_specs=(spec, spec), check_vma=False
    )
```

```python
import functools

import jax
import jax.numpy as jnp
from jax import lax
from jax.experimental import pallas as pl
from jax.experimental.pallas import tpu as pltpu
from jax.sharding import PartitionSpec as P

STEPS = 6
CHUNKS = 8
PIECES = 4
AXES = ("py", "px", "pz")
MESH = pl.DeviceIdType.MESH


def kernel(
    counts, chunks, pieces, density, crowding, odd, even,
    crowd, y_in, x_in, z_in, z_out, total_in, total_out,
    load_sem, y_send, y_recv, face_send, face_recv, total_send, total_recv,
):
    planes, rows, depth, lanes = density.shape
    part = rows // chunks
    bit = part // pieces
    last = planes - 1
    place = [lax.axis_index(axis) for axis in AXES]
    near = []
    for axis, at, count in zip(AXES, place, counts):
        near.append(((at > 0, {axis: at - 1}), (at < count - 1, {axis: at + 1})))
    groups = (pl.ds(0, 1), pl.ds(1, planes - 2), pl.ds(last, 1))

    barrier = pltpu.get_barrier_semaphore()
    awaited = jnp.int32(0)
    for sides in near:
        for there, device in sides:
            awaited = awaited + there.astype(jnp.int32)

            @pl.when(there)
            def _(device=device):
                pl.semaphore_signal(barrier, inc=1, device_id=device, device_id_type=MESH)

    load_field = pltpu.make_async_copy(density, even, load_sem.at[0])
    load_crowd = pltpu.make_async_copy(crowding, crowd, load_sem.at[1])
    load_field.start()
    load_crowd.start()
    pl.semaphore_wait(barrier, awaited)

    def field(level):
        return even if level % 2 == 0 else odd

    def y_copy(level, side, chunk):
        source = density if level == 0 else field(level)
        own = pl.ds(chunk * part, part)
        return pltpu.make_async_remote_copy(
            src_ref=source.at[last if side == 0 else 0, own],
            dst_ref=y_in.at[level, side, own],
            send_sem=y_send.at[level, side, chunk],
            recv_sem=y_recv.at[level, side, chunk],
            device_id=near[0][1 - side][1],
            device_id_type=MESH,
        )

    def face_copy(level, dim, side, group):
        own = groups[group]
        if dim == 1:
            source = density if level == 0 else field(level)
            source, landing = source.at[own, rows - 1 if side == 0 else 0], x_in
        else:
            source, landing = z_out.at[level, side, own], z_in
        slot = (level, (dim - 1) * 2 + side, group)
        return pltpu.make_async_remote_copy(
            src_ref=source,
            dst_ref=landing.at[level, side, own],
            send_sem=face_send.at[slot],
            recv_sem=face_recv.at[slot],
            device_id=near[dim][1 - side][1],
            device_id_type=MESH,
        )

    def total_copy(piece):
        own = pl.ds(piece * bit, bit)
        return pltpu.make_async_remote_copy(
            src_ref=total_out.at[own],
            dst_ref=total_in.at[own],
            send_sem=total_send.at[piece],
            recv_sem=total_recv.at[piece],
            device_id=near[0][1][1],
            device_id_type=MESH,
        )

    def sent_to(dim, side):
        return near[dim][1 - side][0]

    def comes_from(dim, side):
        return near[dim][side][0]

    def when(condition, action):
        pl.when(condition)(action)

    def y_start(level, chunk):
        for side in (0, 1):
            when(sent_to(0, side), lambda side=side: y_copy(level, side, chunk).start())

    def y_wait_send(level, chunk):
        for side in (0, 1):
            when(sent_to(0, side), lambda side=side: y_copy(level, side, chunk).wait_send())

    def y_wait_recv(level, chunk):
        for side in (0, 1):
            when(comes_from(0, side), lambda side=side: y_copy(level, side, chunk).wait_recv())

    def faces(level, some, dims, which, act):
        for dim in dims:
            for side in (0, 1):
                def action(dim=dim, side=side):
                    for group in some:
                        getattr(face_copy(level, dim, side, group), act)()

                when(which(dim, side), action)

    OUTER, INNER, ALL = (0, 2), (1,), (0, 2, 1)

    def over(low, high, body):
        lax.fori_loop(low, high, lambda i, carry: (body(i), carry)[1], 0)

    over(0, chunks, lambda chunk: y_start(0, chunk))
    faces(0, ALL, (1,), sent_to, "start")

    for side in (0, 1):
        @pl.when(jnp.logical_not(comes_from(0, side)))
        def _(side=side):
            def clear(row):
                for level in range(STEPS):
                    y_in[level, side, row] = jnp.zeros((depth, lanes), jnp.float32)
            over(0, rows, clear)

        @pl.when(jnp.logical_not(comes_from(1, side)))
        def _(side=side):
            def clear(plane):
                for level in range(STEPS):
                    x_in[level, side, plane] = jnp.zeros((depth, lanes), jnp.float32)
            over(0, planes, clear)

        @pl.when(jnp.logical_not(comes_from(2, side)))
        def _(side=side):
            def clear(plane):
                for level in range(STEPS):
                    z_in[level, side, plane] = jnp.zeros((rows, lanes), jnp.float32)
            over(0, planes, clear)

    load_field.wait()

    def pack(row):
        for plane in range(planes):
            z_out[0, 1, plane, pl.ds(row, 1)] = even[plane, row, 0:1]
            z_out[0, 0, plane, pl.ds(row, 1)] = even[plane, row, depth - 1:depth]

    over(0, rows, pack)
    faces(0, ALL, (2,), sent_to, "start")
    load_crowd.wait()

    index = lax.broadcasted_iota(jnp.int32, (depth, lanes), 0)
    at_low, at_high = index == 0, index == depth - 1

    def advance(level, plane, row, x_edge):
        now = field(level)
        middle = now[plane, row]
        below = y_in[level, 0, row] if plane == 0 else now[plane - 1, row]
        above = y_in[level, 1, row] if plane == last else now[plane + 1, row]
        before = x_in[level, 0, plane] if x_edge < 0 else now[plane, row - 1]
        after = x_in[level, 1, plane] if x_edge > 0 else now[plane, row + 1]
        down = jnp.where(at_low, z_in[level, 0, plane, pl.ds(row, 1)], pltpu.roll(middle, 1, 0))
        up = jnp.where(at_high, z_in[level, 1, plane, pl.ds(row, 1)], pltpu.roll(middle, depth - 1, 0))
        around = ((below + above) + (before + after)) + (down + up)
        rate = 6.0 - 2.0 * (middle * crowd[plane, row])
        value = 0.1 * (around + middle * rate)
        field(level + 1)[plane, row] = value
        if level + 1 < STEPS:
            z_out[level + 1, 1, plane, pl.ds(row, 1)] = value[0:1]
            z_out[level + 1, 0, plane, pl.ds(row, 1)] = value[depth - 1:depth]
        return value

    def sweep(low, high, body):
        when(low == 0, lambda: body(0, -1))
        over(jnp.maximum(low, 1), jnp.minimum(high, rows - 1), lambda row: body(row, 0))
        when(high == rows, lambda: body(rows - 1, 1))

    for level in range(STEPS - 1):
        faces(level, OUTER, (1, 2), comes_from, "wait_recv")
        if level:
            faces(level - 1, OUTER, (1, 2), sent_to, "wait_send")

        def outer(chunk, level=level):
            y_wait_recv(level, chunk)
            if level:
                y_wait_send(level - 1, chunk)

            def cells(row, x_edge):
                for plane in (0, last):
                    advance(level, plane, row, x_edge)

            sweep(chunk * part, (chunk + 1) * part, cells)
            y_start(level + 1, chunk)

        over(0, chunks, outer)
        faces(level + 1, OUTER, (1, 2), sent_to, "start")

        faces(level, INNER, (1, 2), comes_from, "wait_recv")
        if level:
            faces(level - 1, INNER, (1, 2), sent_to, "wait_send")

        def cells(row, x_edge, level=level):
            for plane in range(1, last):
                advance(level, plane, row, x_edge)

        sweep(jnp.int32(0), jnp.int32(rows), cells)
        faces(level + 1, INNER, (1, 2), sent_to, "start")

    final = STEPS - 1
    faces(final, ALL, (1, 2), comes_from, "wait_recv")
    faces(final - 1, ALL, (1, 2), sent_to, "wait_send")
    first, forwards = jnp.logical_not(near[0][0][0]), near[0][1][0]

    def ending(chunk):
        y_wait_recv(final, chunk)
        y_wait_send(final - 1, chunk)

        def cells(row, x_edge):
            total = advance(final, 0, row, x_edge)
            for plane in range(1, planes):
                total = total + advance(final, plane, row, x_edge)
            total_out[row] = total

        sweep(chunk * part, (chunk + 1) * part, cells)
        when(jnp.logical_and(first, forwards), lambda: over(
            chunk * pieces, (chunk + 1) * pieces, lambda piece: total_copy(piece).start()
        ))

    over(0, chunks, ending)
    faces(final, ALL, (1, 2), sent_to, "wait_send")
    over(0, chunks, lambda chunk: y_wait_send(final, chunk))

    @pl.when(first)
    def _():
        def clear(row):
            total_in[row] = jnp.zeros((depth, lanes), jnp.float32)
        over(0, rows, clear)

    result, scale = odd, 1.0 / (planes * counts[0])

    def summing(piece):
        low, high = piece * bit, (piece + 1) * bit

        @pl.when(jnp.logical_not(first))
        def _():
            total_copy(piece).wait_recv()

            @pl.when(forwards)
            def _():
                def add(row):
                    total_out[row] = total_out[row] + total_in[row]
                over(low, high, add)
                total_copy(piece).start()

        def cells(row):
            running = total_in[row]
            for plane in range(planes):
                running = running + even[plane, row]
                result[plane, row] = running * scale
        over(low, high, cells)

    over(0, chunks * pieces, summing)
    when(forwards, lambda: over(0, chunks * pieces, lambda piece: total_copy(piece).wait_send()))


def store(sums, field, column_sum, density_end, sem):
    planes = sums.shape[0]
    copies = []
    for plane in range(planes):
        for source, target in ((field, density_end), (sums, column_sum)):
            copies.append(pltpu.make_async_copy(source.at[plane], target.at[plane], sem.at[len(copies)]))
            copies[-1].start()
    for copy in copies:
        copy.wait()


def local(mesh, density, crowding):
    planes, rows, depth, lanes = density.shape
    chunks = CHUNKS if rows % CHUNKS == 0 else 1
    pieces = PIECES if (rows // chunks) % PIECES == 0 else 1
    counts = tuple(mesh.shape[axis] for axis in AXES)
    f32 = jnp.float32
    block = (planes, rows, depth, lanes)
    scratch = [
        (block), (STEPS, 2, rows, depth, lanes), (STEPS, 2, planes, depth, lanes),
        (STEPS, 2, planes, rows, lanes), (STEPS, 2, planes, rows, lanes),
        (rows, depth, lanes), (rows, depth, lanes),
    ]
    DMA = pltpu.SemaphoreType.DMA
    cells = planes * rows * depth * lanes
    sums, field = pl.pallas_call(
        functools.partial(kernel, counts, chunks, pieces),
        out_shape=(pltpu.VMEM(block, f32), pltpu.VMEM(block, f32)),
        in_specs=[pl.BlockSpec(memory_space=pltpu.HBM)] * 2,
        out_specs=(pl.BlockSpec(memory_space=pltpu.VMEM), pl.BlockSpec(memory_space=pltpu.VMEM)),
        scratch_shapes=[pltpu.VMEM(shape, f32) for shape in scratch] + [
            DMA((2,)),
            DMA((STEPS, 2, chunks)), DMA((STEPS, 2, chunks)),
            DMA((STEPS, 4, 3)), DMA((STEPS, 4, 3)),
            DMA((chunks * pieces,)), DMA((chunks * pieces,)),
        ],
        compiler_params=pltpu.CompilerParams(
            collective_id=0, has_side_effects=True, vmem_limit_bytes=40 * 2**20
        ),
        cost_estimate=pl.CostEstimate(flops=cells * 66, bytes_accessed=cells * 16, transcendentals=0),
        name="march",
    )(density, crowding)
    return pl.pallas_call(
        store,
        out_shape=(jax.ShapeDtypeStruct(block, f32), jax.ShapeDtypeStruct(block, f32)),
        in_specs=[pl.BlockSpec(memory_space=pltpu.VMEM)] * 2,
        out_specs=(pl.BlockSpec(memory_space=pltpu.HBM), pl.BlockSpec(memory_space=pltpu.HBM)),
        scratch_shapes=[DMA((2 * planes,))],
        compiler_params=pltpu.CompilerParams(vmem_limit_bytes=2**20),
        cost_estimate=pl.CostEstimate(flops=0, bytes_accessed=cells * 8, transcendentals=0),
        name="store",
    )(sums, field)


def solution(mesh):
    spec = P(*AXES, None)
    return jax.shard_map(
        functools.partial(local, mesh), mesh=mesh, in_specs=(spec, spec), out_specs=(spec, spec), check_vma=False
    )
```
